256 devices in a mesh: seq: 32 (over x, y, core), head: 8 (over z).
Axes of the slice: x: 4, y: 4, z: 8, core: 2. Of those that a mesh axis runs over, the one named last changes fastest.
Arguments:
- x_in: bfloat16 [81920, 6144], P('seq', 'head'), may hold values from -6 to 6
- bc_in: bfloat16 [81920, 256], P('seq'), may hold values from -6 to 6
- gate_in: bfloat16 [81920, 6144], P('seq', 'head'), may hold values from -45 to 45
- log_decay: float32 [96, 81920], P('head', 'seq'), may hold values from -2.5 to 0, as said below
- step_size: float32 [96, 81920], P('head', 'seq'), may hold values from 0 to 0.5, as said below
- conv_x: bfloat16 [4, 6144], P(None, 'head'), may hold values from -3 to 3
- conv_bc: bfloat16 [4, 256], replicated, may hold values from -3 to 3
- skip_gain: float32 [96], P('head'), may hold values from 0.1 to 1.9
- norm_gain: float32 [6144], P('head'), may hold values from 0.5 to 1.5
Outputs:
- mamba_out: bfloat16 [81920, 6144], P('seq', 'head')
The draws below stay inside these ranges and needn't reach their ends.
Inputs may be any that keep to these rules, and one draw needn't show every extreme that they name: `log_decay`: negative. `step_size`: positive.
All inputs are finite; a program needn't handle non-finite values.
Results may differ from the reference program's by a relative error of at most 0.0054.
Values may be sent and summed in bfloat16 or wider, within the bound.
A program may use at most 128 MiB of HBM per device.

```python
import math
import jax
import jax.numpy as jnp
from jax import lax

MIXER_HEADS = 96
HP = 64
NS = 128
CONV = 4
BLOCK = 256
TOK_DEV = 2560
TOKEN_COUNT = 81920
INNER = 6144


def rate_fields(key):
    random_subkeys = jax.random.split(jax.random.fold_in(key, 7), 8)
    fast_cut = 0.3
    medium_cut = 0.45
    class_draw = jax.random.uniform(random_subkeys[0], (MIXER_HEADS,))
    fast_rate = jnp.exp(jax.random.uniform(random_subkeys[1], (MIXER_HEADS,), minval=math.log(1.0 / 50.0), maxval=math.log(1.0 / 30.0)))
    medium_rate = jnp.exp(jax.random.uniform(random_subkeys[2], (MIXER_HEADS,), minval=math.log(1.0 / TOK_DEV), maxval=math.log(4.0 / TOK_DEV)))
    slow_rate = jnp.exp(jax.random.uniform(random_subkeys[3], (MIXER_HEADS,), minval=math.log(0.05 / TOKEN_COUNT), maxval=math.log(0.35 / TOKEN_COUNT)))
    per_head_rate = jnp.where(class_draw < fast_cut, fast_rate, jnp.where(class_draw < medium_cut, medium_rate, slow_rate))
    region = jnp.exp(jax.random.uniform(random_subkeys[4], (MIXER_HEADS, TOKEN_COUNT // BLOCK), minval=-math.log(2.0), maxval=math.log(2.0)))
    region_rows = jnp.repeat(region, BLOCK, axis=1)
    jitter = jnp.exp(jax.random.uniform(random_subkeys[5], (MIXER_HEADS, TOKEN_COUNT), minval=-0.35, maxval=0.35))
    multiplier = region_rows * jitter
    spike_position = jax.random.randint(random_subkeys[6], (MIXER_HEADS, 2), 0, TOKEN_COUNT)
    spike_magnitude = jax.random.uniform(random_subkeys[7], (MIXER_HEADS, 2), minval=0.223, maxval=0.693)
    token_positions = jnp.arange(TOKEN_COUNT)
    spike_events = jnp.sum(spike_magnitude[:, :, None] * (token_positions[None, None, :] == spike_position[:, :, None]), axis=1)
    rate_logarithm = -per_head_rate[:, None] * multiplier - spike_events
    step_rows = 0.5 * jnp.sqrt(per_head_rate[:, None] * multiplier)
    return (rate_logarithm.astype(jnp.float32), step_rows.astype(jnp.float32))


def draw_log_decay(key, part):
    return rate_fields(key)[0]


def draw_step_size(key, part):
    return rate_fields(key)[1]


def draw_gate_in(key, part):
    random_subkeys = jax.random.split(jax.random.fold_in(key, 13), 3)
    columns = jnp.arange(INNER).astype(jnp.float32) / INNER
    column_scale = jnp.exp(math.log(10.0) * (0.5 * columns + 0.5 * jax.random.uniform(random_subkeys[0], (INNER,))))
    base_draw = jax.random.truncated_normal(random_subkeys[1], -5.0, 5.0, (TOKEN_COUNT, INNER))
    row_scale = jnp.exp(math.log(3.0) * jax.random.uniform(random_subkeys[2], (TOKEN_COUNT, 1)))
    return (0.25 * base_draw * column_scale[None, :] * row_scale).astype(jnp.bfloat16)


def level_of(stream_key, dims, shards, least, high):
    level, own = 1.0, jax.random.fold_in(stream_key, 6)
    for dim, shards_of in shards:
        steps = jnp.exp(jax.random.uniform(jax.random.fold_in(own, dim), (shards_of,), jnp.float32, least / len(shards), high / len(shards)))
        level = level * jnp.repeat(steps, dims[dim] // shards_of).reshape([-1 if axis == dim else 1 for axis in range(len(dims))])
    return level


def noise(key, shape, deviation, limit, cuts=(), held_as=jnp.bfloat16):
    array = deviation * jax.random.normal(key, shape, jnp.float32)
    if cuts:
        array = array * level_of(key, shape, cuts, -0.22, 0.18)
    return jnp.clip(array, -limit, limit).astype(held_as)


def setup_inputs(seed: int = 0) -> dict:
    arg_keys = jax.random.split(jax.random.key(seed), 10)
    x_in = noise(arg_keys[0], (TOKEN_COUNT, INNER), 1.0, 6.0, ((0, 32), (1, 8)))
    bc_in = noise(arg_keys[1], (TOKEN_COUNT, 2 * NS), 1.0, 6.0, ((0, 32),))
    gate_in = draw_gate_in(jax.random.fold_in(arg_keys[9], 71), 0)
    log_decay = draw_log_decay(jax.random.fold_in(arg_keys[9], 71), 0)
    step_size = draw_step_size(jax.random.fold_in(arg_keys[9], 71), 0)
    conv_x = noise(arg_keys[5], (CONV, INNER), CONV ** -0.5, 3.0, ((1, 8),))
    conv_bc = noise(arg_keys[6], (CONV, 2 * NS), CONV ** -0.5, 3.0)
    skip_gain = jnp.clip(1.0 + 0.18 * jax.random.normal(arg_keys[7], (MIXER_HEADS,), jnp.float32), 0.1, 1.9)
    norm_gain = jnp.clip(1.0 + 0.1 * jax.random.normal(arg_keys[8], (INNER,), jnp.float32), 0.5, 1.5)
    return dict(x_in=x_in, bc_in=bc_in, gate_in=gate_in, log_decay=log_decay, step_size=step_size, conv_x=conv_x, conv_bc=conv_bc, skip_gain=skip_gain, norm_gain=norm_gain)


def conv_silu(seq_rows, kernel):
    row_count = seq_rows.shape[0]
    padded = jnp.pad(seq_rows, ((kernel.shape[0] - 1, 0), (0, 0)))
    running = jnp.zeros((row_count, seq_rows.shape[1]), jnp.float32)
    for offset in range(kernel.shape[0]):
        running = running + padded[offset:offset + row_count].astype(jnp.float32) * kernel[offset].astype(jnp.float32)
    return jax.nn.silu(running).astype(jnp.bfloat16)

def reference(x_in, bc_in, gate_in, log_decay, step_size, conv_x, conv_bc, skip_gain, norm_gain):
    xs_rows = conv_silu(x_in, conv_x)
    bc_rows = conv_silu(bc_in, conv_bc)
    block_count = TOKEN_COUNT // BLOCK
    causal_mask = jnp.arange(BLOCK)[:, None] >= jnp.arange(BLOCK)[None, :]

    def advance(state_now, pieces):
        xs_blk, bc_blk, gate_blk, decay_blk, step_blk = pieces
        b_blk = bc_blk[:, :NS]
        c_blk = bc_blk[:, NS:]
        xs_heads = xs_blk.reshape(BLOCK, MIXER_HEADS, HP)
        cum_decay = jnp.cumsum(decay_blk, axis=1)
        scores = jnp.einsum('in,jn->ij', c_blk.astype(jnp.float32), b_blk.astype(jnp.float32))
        gap = jnp.where(causal_mask[None], cum_decay[:, :, None] - cum_decay[:, None, :], -jnp.inf)
        weights = (scores[None] * jnp.exp(gap) * step_blk[:, None, :]).astype(jnp.bfloat16)
        intra_part = jnp.einsum('hij,jhp->ihp', weights.astype(jnp.float32), xs_heads.astype(jnp.float32))
        carried = jnp.einsum('in,hpn->ihp', c_blk.astype(jnp.float32), state_now, precision=lax.Precision.HIGHEST) * jnp.exp(cum_decay).T[:, :, None]
        tail_factor = jnp.exp(cum_decay[:, -1:] - cum_decay) * step_blk
        weighted = (xs_heads.astype(jnp.float32) * tail_factor.T[:, :, None]).astype(jnp.bfloat16)
        update = jnp.einsum('jhp,jn->hpn', weighted.astype(jnp.float32), b_blk.astype(jnp.float32))
        new_state = jnp.exp(cum_decay[:, -1])[:, None, None] * state_now + update
        mixed_rows = intra_part + carried + skip_gain[None, :, None] * xs_heads.astype(jnp.float32)
        gated_rows = mixed_rows.reshape(BLOCK, INNER) * jax.nn.silu(gate_blk.astype(jnp.float32))
        mean_square = lax.optimization_barrier(jnp.sum(gated_rows * gated_rows, axis=1)) / INNER
        result = (gated_rows * lax.rsqrt(mean_square + 1e-05)[:, None] * norm_gain).astype(jnp.bfloat16)
        return (new_state, result)
    decay_blocks = log_decay.reshape(MIXER_HEADS, block_count, BLOCK).transpose(1, 0, 2)
    step_blocks = step_size.reshape(MIXER_HEADS, block_count, BLOCK).transpose(1, 0, 2)
    start_state = jnp.zeros((MIXER_HEADS, HP, NS), jnp.float32)
    final_state, outputs = lax.scan(advance, start_state, (xs_rows.reshape(block_count, BLOCK, INNER), bc_rows.reshape(block_count, BLOCK, 2 * NS), gate_in.reshape(block_count, BLOCK, INNER), decay_blocks, step_blocks))
    return outputs.reshape(TOKEN_COUNT, INNER)
```

```python
import functools

import jax
import jax.numpy as jnp
from jax import lax
from jax.experimental import pallas as pl
from jax.experimental.pallas import tpu as pltpu
from jax.sharding import PartitionSpec as P

HP = 64
NS = 128
CONV = 4
Q = 128
HALO = 16
PIECES = 32
LOG2E = 1.4426950408889634
F32 = jnp.float32
BF16 = jnp.bfloat16
MESH = pl.DeviceIdType.MESH


def dot(a, b, ca=1, cb=0, precision=None):
    return lax.dot_general(
        a, b, (((ca,), (cb,)), ((), ())), preferred_element_type=F32, precision=precision
    )


def conv_half_silu(window, taps):
    h = None
    for o in range(CONV):
        start = HALO - (CONV - 1) + o
        term = window[start : start + Q] * taps[o : o + 1]
        h = term if h is None else h + term
    return h + h * jnp.tanh(h)


def kernel(
    nseq,
    nhead,
    x_hbm,
    bc_hbm,
    gate_hbm,
    ld_ref,
    dt_ref,
    kx_ref,
    kbc_ref,
    skip_ref,
    gain_ref,
    out_ref,
    xbuf,
    bcbuf,
    gbuf,
    ld16,
    dt16,
    xs_ref,
    bcs_ref,
    y_ref,
    u_ref,
    brow_ref,
    acol_ref,
    colb_ref,
    drow_ref,
    ohe_ref,
    oht_ref,
    oh16_ref,
    tri_ref,
    st_ref,
    dec_all,
    send1,
    recv1,
    send2,
    recv2,
    ss_all,
    in_sem,
    halo_send,
    halo_recv,
    dec_send,
    dec_recv,
    one_send,
    one_recv,
    two_send,
    two_recv,
    ss_send,
    ss_recv,
):
    heads = ld_ref.shape[0]
    rows, width = out_ref.shape
    nc = rows // Q
    half = width // 2
    per = PIECES // nseq
    lanes = width // 128
    groups = ss_send.shape[1]
    gsize = nc // groups
    inner = width * nhead
    me = lax.axis_index("seq")
    mz = lax.axis_index("head")

    def seq_peer(i):
        return lax.rem(me + i, nseq)

    def head_peer(i):
        return lax.rem(mz + i, nhead)

    def in_copies(c):
        at = pl.ds(pl.multiple_of(c * Q, Q), Q)
        to = pl.ds(pl.multiple_of(c * Q + HALO, HALO), Q)
        return (
            pltpu.make_async_copy(x_hbm.at[at], xbuf.at[to], in_sem.at[0, c]),
            pltpu.make_async_copy(bc_hbm.at[at], bcbuf.at[to], in_sem.at[1, c]),
            pltpu.make_async_copy(gate_hbm.at[at], gbuf.at[at], in_sem.at[2, c]),
        )

    def issue_in(i, _):
        c = nc - 1 - i
        copies = in_copies(c)
        copies[0].start()
        copies[1].start()
        return 0

    lax.fori_loop(0, nc, issue_in, 0)

    barrier = pltpu.get_barrier_semaphore()

    def greet_seq(i, _):
        pl.semaphore_signal(barrier, inc=1, device_id={"seq": seq_peer(i)}, device_id_type=MESH)
        return 0

    def greet_head(i, _):
        pl.semaphore_signal(barrier, inc=1, device_id={"head": head_peer(i)}, device_id_type=MESH)
        return 0

    lax.fori_loop(1, nseq, greet_seq, 0)
    lax.fori_loop(1, nhead, greet_head, 0)

    def issue_gate(i, _):
        in_copies(i)[2].start()
        return 0

    lax.fori_loop(0, nc, issue_gate, 0)

    def onehot(shape, picks):
        r = lax.broadcasted_iota(jnp.int32, shape, 0)
        h = lax.broadcasted_iota(jnp.int32, shape, 1) // HP
        hit = r == h + picks[0]
        for p in picks[1:]:
            hit = hit | (r == h + p)
        return jnp.where(hit, 1.0, 0.0)

    ohe_ref[...] = onehot((128, width), (16, 80)).astype(BF16)
    oht_ref[...] = onehot((128, width), (32, 96)).astype(BF16)
    oh16_ref[...] = onehot((16, width), (0,))
    row = lax.broadcasted_iota(jnp.int32, (Q, Q), 0)
    col = lax.broadcasted_iota(jnp.int32, (Q, Q), 1)
    tri_ref[...] = jnp.where(row <= col, 1.0, 0.0)
    ld16[...] = jnp.zeros_like(ld16)
    dt16[...] = jnp.ones_like(dt16)
    ld16[0:heads, :] = ld_ref[...]
    dt16[0:heads, :] = dt_ref[...]

    def spread(column):
        return jnp.sum(oh16_ref[...] * column, axis=0, keepdims=True)

    total = jnp.sum(ld16[...], axis=1, keepdims=True)
    dec_all[me] = spread(jnp.exp(total))
    st_ref[...] = jnp.zeros_like(st_ref)

    def halo_copies():
        peer = {"seq": seq_peer(1)}
        tail = pl.ds(rows, HALO)
        return (
            pltpu.make_async_remote_copy(
                xbuf.at[tail], xbuf.at[pl.ds(0, HALO)], halo_send.at[0], halo_recv.at[0],
                device_id=peer, device_id_type=MESH,
            ),
            pltpu.make_async_remote_copy(
                bcbuf.at[tail], bcbuf.at[pl.ds(0, HALO)], halo_send.at[1], halo_recv.at[1],
                device_id=peer, device_id_type=MESH,
            ),
        )

    def dec_copy(peer, source):
        return pltpu.make_async_remote_copy(
            dec_all.at[source], dec_all.at[source], dec_send.at[peer], dec_recv.at[source],
            device_id={"seq": peer}, device_id_type=MESH,
        )

    def phase_a(i, g):
        c = nc - 1 - i

        @pl.when(i == nc // 2)
        def _():
            pl.semaphore_wait(barrier, nseq - 1 + nhead - 1)
            for copy in halo_copies():
                copy.start()

            def send(k, _):
                dec_copy(seq_peer(k), me).start()
                return 0

            lax.fori_loop(1, nseq, send, 0)

        @pl.when(i < nc - 1)
        def _():
            copies = in_copies(c - 1)
            copies[0].wait()
            copies[1].wait()

        @pl.when(i == nc - 1)
        def _():
            for copy in halo_copies():
                copy.wait_recv()

            @pl.when(me == 0)
            def _():
                xbuf[0:HALO, :] = jnp.zeros((HALO, width), BF16)
                bcbuf[0:HALO, :] = jnp.zeros((HALO, 2 * NS), BF16)

        at = pl.ds(pl.multiple_of(c * Q, Q), Q)
        window = pl.ds(pl.multiple_of(c * Q, Q), Q + HALO)
        step = dt16[:, at]
        cum = dot(ld16[:, at], tri_ref[...], precision=lax.Precision.HIGHEST)
        tot = cum[:, Q - 1 : Q]
        brow_ref[c] = (cum - jnp.log(step)) * LOG2E
        from_start = jnp.exp(cum)
        to_end = jnp.exp(tot - cum) * step
        start_hi = from_start.astype(BF16).astype(F32)
        end_hi = to_end.astype(BF16).astype(F32)
        zero = jnp.zeros((16, Q), F32)
        stack = jnp.concatenate(
            [cum * LOG2E, start_hi, end_hi, zero, zero, from_start - start_hi, to_end - end_hi, zero],
            axis=0,
        ).T
        acol_ref[c] = stack
        stack = stack.astype(BF16)
        colb_ref[c] = stack
        drow_ref[c] = spread(jnp.exp(tot))
        grow = spread(jnp.exp(g))
        taps = kbc_ref[...].astype(F32) * 0.5
        bcs = [
            conv_half_silu(
                bcbuf[window, 128 * j : 128 * j + 128].astype(F32), taps[:, 128 * j : 128 * j + 128]
            ).astype(BF16)
            for j in range(2)
        ]
        bcs_ref[c, :, 0:128] = bcs[0]
        bcs_ref[c, :, 128:256] = bcs[1]
        taps = kx_ref[...].astype(F32) * 0.5
        for j in range(lanes):
            cols = slice(128 * j, 128 * j + 128)
            xs = conv_half_silu(xbuf[window, cols].astype(F32), taps[:, cols])
            xs_ref[c, :, cols] = xs.astype(BF16)
            weighted = (xs * dot(stack, oht_ref[:, cols])).astype(BF16)
            update = dot(bcs[0], weighted, 0, 0)
            u_ref[c, :, cols] = update
            st_ref[:, cols] += grow[:, cols] * update
        return g + tot

    copies = in_copies(nc - 1)
    copies[0].wait()
    copies[1].wait()
    lax.fori_loop(0, nc, phase_a, jnp.zeros((16, 1), F32))

    for q in range(PIECES):
        r, l = q // 2, q % 2
        send1[q // per, q % per] = st_ref[8 * r : 8 * r + 8, half * l : half * l + half].astype(BF16)
    recv1[me] = send1[me]

    def one_copy(peer, source):
        return pltpu.make_async_remote_copy(
            send1.at[peer], recv1.at[source], one_send.at[peer], one_recv.at[source],
            device_id={"seq": peer}, device_id_type=MESH,
        )

    def two_copy(peer, source):
        return pltpu.make_async_remote_copy(
            send2.at[peer], recv2.at[source], two_send.at[peer], two_recv.at[source],
            device_id={"seq": peer}, device_id_type=MESH,
        )

    def send_one(k, _):
        one_copy(seq_peer(k), me).start()
        return 0

    lax.fori_loop(1, nseq, send_one, 0)

    def second_round():
        def arrived(k, _):
            peer = seq_peer(k)
            dec_copy(peer, peer).wait_recv()
            one_copy(peer, peer).wait_recv()
            return 0

        lax.fori_loop(1, nseq, arrived, 0)
        for e in range(per):
            l = lax.rem(me * per + e, 2)
            cols = pl.ds(pl.multiple_of(l * half, 128), half)

            def scan(k, acc):
                send2[k, e] = acc.astype(BF16)
                return dec_all[k, :, cols] * acc + recv1[k, e].astype(F32)

            lax.fori_loop(0, nseq, scan, jnp.zeros((8, half), F32))
        recv2[me] = send2[me]

        def send_two(k, _):
            two_copy(seq_peer(k), me).start()
            return 0

        lax.fori_loop(1, nseq, send_two, 0)

    lane = lax.broadcasted_iota(jnp.int32, (Q, 128), 1)
    lower = lax.broadcasted_iota(jnp.int32, (Q, Q), 0) >= lax.broadcasted_iota(jnp.int32, (Q, Q), 1)

    def phase_b(c, _):
        @pl.when(c == nc // 2)
        def _():
            second_round()

        scores = jnp.where(lower, dot(bcs_ref[c, :, 128:256], bcs_ref[c, :, 0:128], 1, 1), 0.0)
        for j in range(lanes):
            cols = slice(128 * j, 128 * j + 128)
            weights = []
            for h in (2 * j, 2 * j + 1):
                gap = acol_ref[c, :, h : h + 1] - brow_ref[c, h : h + 1, :]
                weights.append((scores * jnp.exp2(jnp.minimum(gap, 0.0))).astype(BF16))
            xs = xs_ref[c, :, cols]
            pair = jnp.concatenate(
                [jnp.where(lane < HP, xs, 0.0).astype(BF16), jnp.where(lane < HP, 0.0, xs).astype(BF16)],
                axis=0,
            )
            intra = dot(jnp.concatenate(weights, axis=1), pair)
            skip = jnp.where(lane < HP, skip_ref[2 * j], skip_ref[2 * j + 1])
            y_ref[c, :, cols] = intra + skip * xs.astype(F32)
        return 0

    lax.fori_loop(0, nc, phase_b, 0)

    def arrived_two(k, _):
        peer = seq_peer(k)
        two_copy(peer, peer).wait_recv()
        return 0

    lax.fori_loop(1, nseq, arrived_two, 0)
    for q in range(PIECES):
        r, l = q // 2, q % 2
        st_ref[8 * r : 8 * r + 8, half * l : half * l + half] = recv2[q // per, q % per].astype(F32)

    def ss_copy(peer, source, g):
        part = pl.ds(g * gsize, gsize)
        return pltpu.make_async_remote_copy(
            ss_all.at[source, part], ss_all.at[source, part],
            ss_send.at[peer, g], ss_recv.at[source, g],
            device_id={"head": peer}, device_id_type=MESH,
        )

    def phase_c(c, _):
        in_copies(c)[2].wait()
        at = pl.ds(pl.multiple_of(c * Q, Q), Q)
        ss = None
        for j in range(lanes):
            cols = slice(128 * j, 128 * j + 128)
            state = st_ref[:, cols]
            carried = dot(bcs_ref[c, :, 128:256], state.astype(BF16))
            st_ref[:, cols] = drow_ref[c, :, cols] * state + u_ref[c, :, cols]
            mixed = y_ref[c, :, cols] + carried * dot(colb_ref[c], ohe_ref[:, cols])
            h = gbuf[at, cols].astype(F32) * 0.5
            gated = mixed * (h + h * jnp.tanh(h))
            y_ref[c, :, cols] = gated
            part = dot(jnp.ones((8, 128), BF16), (gated * gated).astype(BF16), 1, 1)
            ss = part if ss is None else ss + part
        ss_all[mz, c] = ss[0:1]
        return 0

    for g in range(groups):
        lax.fori_loop(g * gsize, (g + 1) * gsize, phase_c, 0)

        def send_ss(k, _):
            ss_copy(head_peer(k), mz, g).start()
            return 0

        lax.fori_loop(1, nhead, send_ss, 0)

    eye = lax.broadcasted_iota(jnp.int32, (Q, Q), 0) == lax.broadcasted_iota(jnp.int32, (Q, Q), 1)

    def phase_d(c, _):
        square = ss_all[0, c]
        for p in range(1, nhead):
            square = square + ss_all[p, c]
        scale = lax.rsqrt(square * (1.0 / inner) + 1e-05)
        scale = jnp.sum(jnp.where(eye, scale, 0.0), axis=1, keepdims=True)
        at = pl.ds(pl.multiple_of(c * Q, Q), Q)
        for j in range(lanes):
            cols = slice(128 * j, 128 * j + 128)
            out_ref[at, cols] = (y_ref[c, :, cols] * scale * gain_ref[:, cols]).astype(BF16)
        return 0

    for g in range(groups):

        def arrived_ss(k, _):
            peer = head_peer(k)
            ss_copy(peer, peer, g).wait_recv()
            return 0

        lax.fori_loop(1, nhead, arrived_ss, 0)
        lax.fori_loop(g * gsize, (g + 1) * gsize, phase_d, 0)

    for copy in halo_copies():
        copy.wait_send()

    def left_seq(k, _):
        peer = seq_peer(k)
        dec_copy(peer, me).wait_send()
        one_copy(peer, me).wait_send()
        two_copy(peer, me).wait_send()
        return 0

    lax.fori_loop(1, nseq, left_seq, 0)

    def left_head(k, _):
        for g in range(groups):
            ss_copy(head_peer(k), mz, g).wait_send()
        return 0

    lax.fori_loop(1, nhead, left_head, 0)


def per_device(nseq, nhead, x_in, bc_in, gate_in, log_decay, step_size, conv_x, conv_bc, skip_gain, norm_gain):
    rows, width = x_in.shape
    nc = rows // Q
    per = PIECES // nseq
    half = width // 2
    groups = 2
    vmem = pl.BlockSpec(memory_space=pltpu.VMEM)
    anywhere = pl.BlockSpec(memory_space=pl.ANY)
    dma = pltpu.SemaphoreType.DMA
    return pl.pallas_call(
        functools.partial(kernel, nseq, nhead),
        out_shape=jax.ShapeDtypeStruct((rows, width), BF16),
        in_specs=[
            anywhere, anywhere, anywhere, vmem, vmem, vmem, vmem,
            pl.BlockSpec(memory_space=pltpu.SMEM), vmem,
        ],
        out_specs=vmem,
        scratch_shapes=[
            pltpu.VMEM((HALO + rows, width), BF16),
            pltpu.VMEM((HALO + rows, 2 * NS), BF16),
            pltpu.VMEM((rows, width), BF16),
            pltpu.VMEM((16, rows), F32),
            pltpu.VMEM((16, rows), F32),
            pltpu.VMEM((nc, Q, width), BF16),
            pltpu.VMEM((nc, Q, 2 * NS), BF16),
            pltpu.VMEM((nc, Q, width), F32),
            pltpu.VMEM((nc, NS, width), F32),
            pltpu.VMEM((nc, 16, Q), F32),
            pltpu.VMEM((nc, Q, 128), F32),
            pltpu.VMEM((nc, Q, 128), BF16),
            pltpu.VMEM((nc, 1, width), F32),
            pltpu.VMEM((128, width), BF16),
            pltpu.VMEM((128, width), BF16),
            pltpu.VMEM((16, width), F32),
            pltpu.VMEM((Q, Q), F32),
            pltpu.VMEM((NS, width), F32),
            pltpu.VMEM((nseq, 1, width), F32),
            pltpu.VMEM((nseq, per, 8, half), BF16),
            pltpu.VMEM((nseq, per, 8, half), BF16),
            pltpu.VMEM((nseq, per, 8, half), BF16),
            pltpu.VMEM((nseq, per, 8, half), BF16),
            pltpu.VMEM((nhead, nc, 1, Q), F32),
            dma((3, nc)),
            dma((2,)), dma((2,)),
            dma((nseq,)), dma((nseq,)),
            dma((nseq,)), dma((nseq,)),
            dma((nseq,)), dma((nseq,)),
            dma((nhead, groups)), dma((nhead, groups)),
        ],
        compiler_params=pltpu.CompilerParams(
            collective_id=0, has_side_effects=True, vmem_limit_bytes=60 * 1024 * 1024
        ),
        name="mamba",
    )(
        x_in, bc_in, gate_in, log_decay, step_size, conv_x, conv_bc, skip_gain,
        norm_gain.reshape(1, width),
    )


def solution(mesh):
    in_specs = (
        P("seq", "head"),
        P("seq", None),
        P("seq", "head"),
        P("head", "seq"),
        P("head", "seq"),
        P(None, "head"),
        P(),
        P("head"),
        P("head"),
    )
    return jax.shard_map(
        functools.partial(per_device, mesh.shape["seq"], mesh.shape["head"]),
        mesh=mesh,
        in_specs=in_specs,
        out_specs=P("seq", "head"),
        check_vma=False,
    )
```

```python
import functools

import jax
import jax.numpy as jnp
from jax import lax
from jax.experimental import pallas as pl
from jax.experimental.pallas import tpu as pltpu
from jax.sharding import PartitionSpec as P

HP = 64
NS = 128
CONV = 4
Q = 128
HALO = 16
PIECES = 32
IN_PIECES = 5
GREET_PIECE = 2
UNROLL_B = 1
VMEM_LIMIT = 56 * 1024 * 1024
LOG2E = 1.4426950408889634
F32 = jnp.float32
BF16 = jnp.bfloat16
MESH = pl.DeviceIdType.MESH


def dot(a, b, ca=1, cb=0, precision=None):
    return lax.dot_general(
        a, b, (((ca,), (cb,)), ((), ())), preferred_element_type=F32, precision=precision
    )


def conv_half_silu(window, taps, shift):
    shift[...] = window[HALO - 8 :].astype(F32)
    h = None
    for o in range(CONV):
        start = 8 - (CONV - 1) + o
        term = shift[start : start + Q] * taps[o : o + 1]
        h = term if h is None else h + term
    return h + h * jnp.tanh(h)


def kernel(
    nseq,
    nhead,
    x_hbm,
    bc_hbm,
    gate_hbm,
    ld_hbm,
    dt_hbm,
    kx_hbm,
    kbc_hbm,
    skip_hbm,
    gain_hbm,
    out_ref,
    ld_ref,
    dt_ref,
    kx_ref,
    kbc_ref,
    skip_ref,
    xbuf,
    bcbuf,
    gbuf,
    ldc,
    dtc,
    start_ref,
    tot_ref,
    xs_ref,
    bcs_ref,
    y_ref,
    gain_ref,
    u_ref,
    brow_ref,
    acol_ref,
    sg_ref,
    colb_ref,
    drow_ref,
    grow_ref,
    ohe_ref,
    oht_ref,
    ohw_ref,
    tri_ref,
    st_ref,
    shift_ref,
    into_ref,
    intob_ref,
    dec_all,
    send1,
    recv1,
    send2,
    recv2,
    ss_all,
    in_sem,
    small_sem,
    halo_send,
    halo_recv,
    dec_send,
    dec_recv,
    one_send,
    one_recv,
    two_send,
    two_recv,
    ss_send,
    ss_recv,
):
    heads = ld_ref.shape[0]
    rows, width = out_ref.shape
    nc = rows // Q
    half = width // 2
    per = PIECES // nseq
    lanes = width // 128
    groups = ((0, nc - nc // 5), (nc - nc // 5, nc))
    inner = width * nhead
    me = lax.axis_index("seq")
    mz = lax.axis_index("head")

    def seq_peer(i):
        return lax.rem(me + i, nseq)

    def head_peer(i):
        return lax.rem(mz + i, nhead)

    piece = rows // IN_PIECES
    blocks = nc // IN_PIECES

    def in_copies(k):
        at = pl.ds(pl.multiple_of(k * piece, piece), piece)
        to = pl.ds(pl.multiple_of(k * piece + HALO, HALO), piece)
        return (
            pltpu.make_async_copy(x_hbm.at[at], xbuf.at[to], in_sem.at[0, k]),
            pltpu.make_async_copy(bc_hbm.at[at], bcbuf.at[to], in_sem.at[1, k]),
        )

    gate_copy = pltpu.make_async_copy(gate_hbm, gbuf, in_sem.at[2, 0])

    small = [
        pltpu.make_async_copy(source, target, small_sem.at[k])
        for k, (source, target) in enumerate(
            [(ld_hbm, ld_ref), (dt_hbm, dt_ref), (kx_hbm, kx_ref), (kbc_hbm, kbc_ref), (skip_hbm, skip_ref), (gain_hbm, gain_ref)]
        )
    ]
    for copy in small:
        copy.start()
    for k in reversed(range(IN_PIECES)):
        for copy in in_copies(k):
            copy.start()

    barrier = pltpu.get_barrier_semaphore()

    def greet_seq(i, _):
        pl.semaphore_signal(barrier, inc=1, device_id={"seq": seq_peer(i)}, device_id_type=MESH)
        return 0

    def greet_head(i, _):
        pl.semaphore_signal(barrier, inc=1, device_id={"head": head_peer(i)}, device_id_type=MESH)
        return 0

    lax.fori_loop(1, nseq, greet_seq, 0)
    lax.fori_loop(1, nhead, greet_head, 0)

    gate_copy.start()

    def onehot(shape, picks):
        r = lax.broadcasted_iota(jnp.int32, shape, 0)
        h = lax.broadcasted_iota(jnp.int32, shape, 1) // HP
        hit = r == h + picks[0]
        for p in picks[1:]:
            hit = hit | (r == h + p)
        return jnp.where(hit, 1.0, 0.0)

    ohe_ref[...] = onehot((128, width), (16, 80)).astype(BF16)
    oht_ref[...] = onehot((128, width), (32, 96)).astype(BF16)
    ohw_ref[...] = onehot((128, width), (48, 64)).astype(BF16)
    row = lax.broadcasted_iota(jnp.int32, (Q, Q), 0)
    col = lax.broadcasted_iota(jnp.int32, (Q, Q), 1)
    tri_ref[...] = jnp.where(row <= col, 1.0, 0.0)
    tops = lax.broadcasted_iota(jnp.int32, (24, 24), 0)
    rests = lax.broadcasted_iota(jnp.int32, (24, 24), 1)
    later = jnp.where((rests > tops) & (rests < nc), 1.0, 0.0)
    ldc[...] = jnp.zeros_like(ldc)
    dtc[...] = jnp.ones_like(dtc)
    tot_ref[...] = jnp.zeros_like(tot_ref)
    for copy in small:
        copy.wait()
    for c in range(nc):
        at = slice(c * Q, c * Q + Q)
        ldc[16 * c : 16 * c + heads, :] = ld_ref[:, at]
        dtc[16 * c : 16 * c + heads, :] = dt_ref[:, at]

    cum = dot(ldc[...], tri_ref[...], precision=lax.Precision.HIGHEST)
    step = dtc[...]
    tot = cum[:, Q - 1 : Q]
    brow_ref[...] = (cum - jnp.log(step)) * LOG2E
    ldc[...] = cum * LOG2E
    from_start = jnp.exp(cum)
    to_end = jnp.exp(tot - cum) * step
    start_ref[...] = from_start
    dtc[...] = to_end

    def turn(c, base):
        at = pl.ds(pl.multiple_of(16 * c, 16), 16)
        first, last = start_ref[at, :], dtc[at, :]
        first_hi = first.astype(BF16).astype(F32)
        last_hi = last.astype(BF16).astype(F32)
        power = ldc[at, :]
        whole = jnp.exp2(power + base)
        whole_hi = whole.astype(BF16).astype(F32)
        stack = jnp.concatenate(
            [
                power, first_hi, last_hi, whole_hi, whole - whole_hi, first - first_hi, last - last_hi,
                jnp.zeros((16, Q), F32),
            ],
            axis=0,
        ).T
        acol_ref[c] = stack
        colb_ref[c] = stack.astype(BF16)
        tot_ref[pl.ds(c, 1), :] = stack[Q - 1 : Q, :]
        return base + power[:, Q - 1 : Q]

    lax.fori_loop(0, nc, turn, jnp.zeros((16, 1), F32), unroll=5)

    heads_only = lax.broadcasted_iota(jnp.int32, (24, 128), 1) < 16
    totals = jnp.where(heads_only, tot_ref[...], 0.0)
    ohf = onehot((128, width), (0,))

    def expand(powers):
        return dot(jnp.exp2(powers), ohf, precision=lax.Precision.HIGHEST)

    drow_ref[...] = expand(totals)
    grow_ref[...] = expand(dot(later, totals, precision=lax.Precision.HIGHEST))
    dec_all[me] = expand(jnp.sum(totals, axis=0, keepdims=True) + jnp.zeros((8, 128), F32))[0:1]
    st_ref[...] = jnp.zeros_like(st_ref)

    def halo_copies():
        peer = {"seq": seq_peer(1)}
        tail = pl.ds(rows, HALO)
        return (
            pltpu.make_async_remote_copy(
                xbuf.at[tail], xbuf.at[pl.ds(0, HALO)], halo_send.at[0], halo_recv.at[0],
                device_id=peer, device_id_type=MESH,
            ),
            pltpu.make_async_remote_copy(
                bcbuf.at[tail], bcbuf.at[pl.ds(0, HALO)], halo_send.at[1], halo_recv.at[1],
                device_id=peer, device_id_type=MESH,
            ),
        )

    def dec_copy(peer, source):
        return pltpu.make_async_remote_copy(
            dec_all.at[source], dec_all.at[source], dec_send.at[peer], dec_recv.at[source],
            device_id={"seq": peer}, device_id_type=MESH,
        )

    def phase_a(c, side):
        window = pl.ds(pl.multiple_of(c * Q, Q), Q + HALO)
        stack = colb_ref[c]
        grow = grow_ref[pl.ds(c, 1), :]
        taps = kbc_ref[...].astype(F32) * 0.5
        bcs = [
            conv_half_silu(
                bcbuf[window, 128 * j : 128 * j + 128], taps[:, 128 * j : 128 * j + 128],
                shift_ref.at[side, lanes + j],
            ).astype(BF16)
            for j in range(2)
        ]
        bcs_ref[c, :, 0:128] = bcs[0]
        bcs_ref[c, :, 128:256] = bcs[1]
        taps = kx_ref[...].astype(F32) * 0.5
        for j in range(0, lanes, 2):
            wide = slice(128 * j, 128 * j + 256)
            ends = dot(stack, oht_ref[:, wide])
            weighted = []
            for t in range(2):
                cols = slice(128 * (j + t), 128 * (j + t) + 128)
                xs = conv_half_silu(xbuf[window, cols], taps[:, cols], shift_ref.at[side, j + t])
                xs_ref[c, :, cols] = xs.astype(BF16)
                weighted.append((xs * ends[:, 128 * t : 128 * t + 128]).astype(BF16))
            update = dot(bcs[0], jnp.concatenate(weighted, axis=1), 0, 0)
            u_ref[c, :, wide] = update
            st_ref[:, wide] += grow[:, wide] * update

    def piece_a(i, _):
        k = IN_PIECES - 1 - i

        @pl.when(k > 0)
        def _():
            for copy in in_copies(k - 1):
                copy.wait()

        @pl.when(i == GREET_PIECE)
        def _():
            pl.semaphore_wait(barrier, nseq - 1 + nhead - 1)
            for copy in halo_copies():
                copy.start()

            def send(k, _):
                dec_copy(seq_peer(k), me).start()
                return 0

            lax.fori_loop(1, nseq, send, 0)

        @pl.when(k == 0)
        def _():
            for copy in halo_copies():
                copy.wait_recv()

            @pl.when(me == 0)
            def _():
                xbuf[0:HALO, :] = jnp.zeros((HALO, width), BF16)
                bcbuf[0:HALO, :] = jnp.zeros((HALO, 2 * NS), BF16)

        def block(b, _):
            for side in range(2):
                phase_a(k * blocks + blocks - 1 - 2 * b - side, side)
            return 0

        lax.fori_loop(0, blocks // 2, block, 0)
        return 0

    for copy in in_copies(IN_PIECES - 1):
        copy.wait()
    lax.fori_loop(0, IN_PIECES, piece_a, 0)

    for q in range(PIECES):
        r, l = q // 2, q % 2
        send1[q // per, q % per] = st_ref[8 * r : 8 * r + 8, half * l : half * l + half].astype(BF16)
    recv1[me] = send1[me]

    def one_copy(peer, source):
        return pltpu.make_async_remote_copy(
            send1.at[peer], recv1.at[source], one_send.at[peer], one_recv.at[source],
            device_id={"seq": peer}, device_id_type=MESH,
        )

    def two_copy(peer, source):
        return pltpu.make_async_remote_copy(
            send2.at[peer], recv2.at[source], two_send.at[peer], two_recv.at[source],
            device_id={"seq": peer}, device_id_type=MESH,
        )

    def send_one(k, _):
        one_copy(seq_peer(k), me).start()
        return 0

    lax.fori_loop(1, nseq, send_one, 0)

    def second_round():
        def arrived(k, _):
            peer = seq_peer(k)
            dec_copy(peer, peer).wait_recv()
            one_copy(peer, peer).wait_recv()
            return 0

        lax.fori_loop(1, nseq, arrived, 0)
        for e in range(per):
            l = lax.rem(me * per + e, 2)
            cols = pl.ds(pl.multiple_of(l * half, 128), half)

            def scan(k, acc):
                send2[k, e] = acc.astype(BF16)
                return dec_all[k, :, cols] * acc + recv1[k, e].astype(F32)

            lax.fori_loop(0, nseq, scan, jnp.zeros((8, half), F32))
        recv2[me] = send2[me]

        def send_two(k, _):
            two_copy(seq_peer(k), me).start()
            return 0

        lax.fori_loop(1, nseq, send_two, 0)

    lane = lax.broadcasted_iota(jnp.int32, (Q, 128), 1)
    left = jnp.where(lane < HP, 1.0, 0.0).astype(BF16)
    right = jnp.where(lane < HP, 0.0, 1.0).astype(BF16)
    lower = lax.broadcasted_iota(jnp.int32, (Q, Q), 0) >= lax.broadcasted_iota(jnp.int32, (Q, Q), 1)

    def phase_b(c, _):
        drow = drow_ref[pl.ds(c, 1), :]
        at = pl.ds(pl.multiple_of(c * Q, Q), Q)
        scores = jnp.where(lower, dot(bcs_ref[c, :, 128:256], bcs_ref[c, :, 0:128], 1, 1), 0.0)
        for j in range(lanes):
            cols = slice(128 * j, 128 * j + 128)
            weights = []
            for h in (2 * j, 2 * j + 1):
                gap = acol_ref[c, :, h : h + 1] - brow_ref[pl.ds(16 * c + h, 1), :]
                weights.append((scores * jnp.exp2(jnp.minimum(gap, 0.0))).astype(BF16))
            xs = xs_ref[c, :, cols]
            pair = jnp.concatenate([xs * left, xs * right], axis=0)
            intra = dot(jnp.concatenate(weights, axis=1), pair)
            skip = jnp.where(lane < HP, skip_ref[2 * j], skip_ref[2 * j + 1])
            state = st_ref[:, cols]
            st_ref[:, cols] = drow[:, cols] * state + u_ref[c, :, cols]
            if j % 2 == 0:
                wide = slice(128 * j, 128 * j + 256)
                decays = dot(colb_ref[c], ohe_ref[:, wide])
                before = []
            before.append(state.astype(BF16))
            y = intra + skip * xs.astype(F32)
            if j % 2 == 1:
                carried = dot(bcs_ref[c, :, 128:256], jnp.concatenate(before, axis=1)) * decays
                y_ref[c, :, 128 * j - 128 : 128 * j] = held + carried[:, :128]
                y_ref[c, :, cols] = y + carried[:, 128:]
            held = y
            h = (gbuf[at, cols] * jnp.asarray(0.5, BF16)).astype(F32)
            sg_ref[c, :, cols] = h + h * jnp.tanh(h)
        return 0

    gate_copy.wait()
    st_ref[...] = jnp.zeros_like(st_ref)
    split = nc // 4 * 2
    lax.fori_loop(0, split, phase_b, 0, unroll=UNROLL_B)
    second_round()
    lax.fori_loop(split, nc, phase_b, 0, unroll=UNROLL_B)

    def arrived_two(k, _):
        peer = seq_peer(k)
        two_copy(peer, peer).wait_recv()
        return 0

    lax.fori_loop(1, nseq, arrived_two, 0)
    for q in range(PIECES):
        r, l = q // 2, q % 2
        into_ref[8 * r : 8 * r + 8, half * l : half * l + half] = recv2[q // per, q % per].astype(F32)
    intob_ref[...] = into_ref[...].astype(BF16)

    def ss_copy(peer, source, g):
        part = pl.ds(groups[g][0], groups[g][1] - groups[g][0])
        return pltpu.make_async_remote_copy(
            ss_all.at[source, part], ss_all.at[source, part],
            ss_send.at[peer, g], ss_recv.at[source, g],
            device_id={"head": peer}, device_id_type=MESH,
        )

    def phase_c(i, _):
        both = pl.ds(2 * i, 2)
        cs = bcs_ref[both, :, 128:256].reshape(2 * Q, 128)
        columns = colb_ref[both].reshape(2 * Q, 128)
        ss = None
        for j in range(0, lanes, 2):
            wide = slice(128 * j, 128 * j + 256)
            carried = dot(cs, intob_ref[:, wide]) * dot(columns, ohw_ref[:, wide])
            mixed = y_ref[both, :, wide].reshape(2 * Q, 256) + carried
            gated = mixed * sg_ref[both, :, wide].reshape(2 * Q, 256)
            u_ref[both, :, wide] = gated.reshape(2, Q, 256)
            square = gated * gated
            part = square[:, :128] + square[:, 128:]
            ss = part if ss is None else ss + part
        ss = ss.astype(BF16)
        for t in range(2):
            ss_all[mz, 2 * i + t] = dot(jnp.ones((8, 128), BF16), ss[Q * t : Q * t + Q], 1, 1)[0:1]
        return 0

    for g in range(len(groups)):
        lax.fori_loop(groups[g][0] // 2, groups[g][1] // 2, phase_c, 0)

        def send_ss(k, _):
            ss_copy(head_peer(k), mz, g).start()
            return 0

        lax.fori_loop(1, nhead, send_ss, 0)

    eye = lax.broadcasted_iota(jnp.int32, (Q, Q), 0) == lax.broadcasted_iota(jnp.int32, (Q, Q), 1)
    gain = gain_ref[...].reshape(1, width)

    def phase_d(c, _):
        square = ss_all[0, c]
        for p in range(1, nhead):
            square = square + ss_all[p, c]
        scale = lax.rsqrt(square * (1.0 / inner) + 1e-05)
        scale = jnp.sum(jnp.where(eye, scale, 0.0), axis=1, keepdims=True)
        at = pl.ds(pl.multiple_of(c * Q, Q), Q)
        for j in range(lanes):
            cols = slice(128 * j, 128 * j + 128)
            out_ref[at, cols] = (u_ref[c, :, cols] * scale * gain[:, cols]).astype(BF16)
        return 0

    for g in range(len(groups)):

        def arrived_ss(k, _):
            peer = head_peer(k)
            ss_copy(peer, peer, g).wait_recv()
            return 0

        lax.fori_loop(1, nhead, arrived_ss, 0)
        lax.fori_loop(*groups[g], phase_d, 0, unroll=2)

    for copy in halo_copies():
        copy.wait_send()

    def left_seq(k, _):
        peer = seq_peer(k)
        dec_copy(peer, me).wait_send()
        one_copy(peer, me).wait_send()
        two_copy(peer, me).wait_send()
        return 0

    lax.fori_loop(1, nseq, left_seq, 0)

    def left_head(k, _):
        for g in range(len(groups)):
            ss_copy(head_peer(k), mz, g).wait_send()
        return 0

    lax.fori_loop(1, nhead, left_head, 0)


def per_device(nseq, nhead, x_in, bc_in, gate_in, log_decay, step_size, conv_x, conv_bc, skip_gain, norm_gain):
    rows, width = x_in.shape
    heads = log_decay.shape[0]
    nc = rows // Q
    per = PIECES // nseq
    half = width // 2
    groups = 2
    vmem = pl.BlockSpec(memory_space=pltpu.VMEM)
    dma = pltpu.SemaphoreType.DMA
    return pl.pallas_call(
        functools.partial(kernel, nseq, nhead),
        out_shape=pltpu.VMEM((rows, width), BF16),
        in_specs=[pl.BlockSpec(memory_space=pltpu.HBM)] * 9,
        out_specs=vmem,
        scratch_shapes=[
            pltpu.VMEM((heads, rows), F32),
            pltpu.VMEM((heads, rows), F32),
            pltpu.VMEM((CONV, width), BF16),
            pltpu.VMEM((CONV, 2 * NS), BF16),
            pltpu.SMEM((heads,), F32),
            pltpu.VMEM((HALO + rows, width), BF16),
            pltpu.VMEM((HALO + rows, 2 * NS), BF16),
            pltpu.VMEM((rows, width), BF16),
            pltpu.VMEM((16 * nc, Q), F32),
            pltpu.VMEM((16 * nc, Q), F32),
            pltpu.VMEM((16 * nc, Q), F32),
            pltpu.VMEM((24, 128), F32),
            pltpu.VMEM((nc, Q, width), BF16),
            pltpu.VMEM((nc, Q, 2 * NS), BF16),
            pltpu.VMEM((nc, Q, width), F32),
            pltpu.VMEM((width,), F32),
            pltpu.VMEM((nc, NS, width), F32),
            pltpu.VMEM((16 * nc, Q), F32),
            pltpu.VMEM((nc, Q, 128), F32),
            pltpu.VMEM((nc, Q, width), F32),
            pltpu.VMEM((nc, Q, 128), BF16),
            pltpu.VMEM((24, width), F32),
            pltpu.VMEM((24, width), F32),
            pltpu.VMEM((128, width), BF16),
            pltpu.VMEM((128, width), BF16),
            pltpu.VMEM((128, width), BF16),
            pltpu.VMEM((Q, Q), F32),
            pltpu.VMEM((NS, width), F32),
            pltpu.VMEM((2, width // 128 + 2, Q + 8, 128), F32),
            pltpu.VMEM((NS, width), F32),
            pltpu.VMEM((NS, width), BF16),
            pltpu.VMEM((nseq, 1, width), F32),
            pltpu.VMEM((nseq, per, 8, half), BF16),
            pltpu.VMEM((nseq, per, 8, half), BF16),
            pltpu.VMEM((nseq, per, 8, half), BF16),
            pltpu.VMEM((nseq, per, 8, half), BF16),
            pltpu.VMEM((nhead, nc, 1, Q), F32),
            dma((3, IN_PIECES)),
            dma((6,)),
            dma((2,)), dma((2,)),
            dma((nseq,)), dma((nseq,)),
            dma((nseq,)), dma((nseq,)),
            dma((nseq,)), dma((nseq,)),
            dma((nhead, groups)), dma((nhead, groups)),
        ],
        compiler_params=pltpu.CompilerParams(
            collective_id=0, has_side_effects=True, vmem_limit_bytes=VMEM_LIMIT
        ),
        name="mamba",
    )(
        *(
            pltpu.with_memory_space_constraint(a, pltpu.HBM)
            for a in (x_in, bc_in, gate_in, log_decay, step_size, conv_x, conv_bc, skip_gain, norm_gain)
        )
    )


def solution(mesh):
    in_specs = (
        P("seq", "head"),
        P("seq", None),
        P("seq", "head"),
        P("head", "seq"),
        P("head", "seq"),
        P(None, "head"),
        P(),
        P("head"),
        P("head"),
    )
    return jax.shard_map(
        functools.partial(per_device, mesh.shape["seq"], mesh.shape["head"]),
        mesh=mesh,
        in_specs=in_specs,
        out_specs=P("seq", "head"),
        check_vma=False,
    )
```

```python
import functools

import jax
import jax.numpy as jnp
from jax import lax
from jax.experimental import pallas as pl
from jax.experimental.pallas import tpu as pltpu
from jax.sharding import PartitionSpec as P

HP = 64
NS = 128
CONV = 4
Q = 128
HALO = 16
PIECES = 32
IN_PIECES = 5
GREET_PIECE = 2
VMEM_LIMIT = 56 * 1024 * 1024
LOG2E = 1.4426950408889634
F32 = jnp.float32
BF16 = jnp.bfloat16
MESH = pl.DeviceIdType.MESH


def dot(a, b, ca=1, cb=0, precision=None):
    return lax.dot_general(
        a, b, (((ca,), (cb,)), ((), ())), preferred_element_type=F32, precision=precision
    )


def thirds(a):
    hi = a.astype(BF16)
    rest = a - hi.astype(F32)
    mid = rest.astype(BF16)
    return hi, mid, (rest - mid.astype(F32)).astype(BF16)


def conv_half_silu(window, taps, shift):
    shift[...] = window[HALO - 8 :].astype(F32)
    h = None
    for o in range(CONV):
        start = 8 - (CONV - 1) + o
        term = shift[start : start + Q] * taps[o : o + 1]
        h = term if h is None else h + term
    return h + h * jnp.tanh(h)


def kernel(
    nseq,
    nhead,
    x_hbm,
    bc_hbm,
    gate_hbm,
    ld_hbm,
    dt_hbm,
    kx_hbm,
    kbc_hbm,
    skip_hbm,
    gain_hbm,
    out_ref,
    ld_ref,
    dt_ref,
    kx_ref,
    kbc_ref,
    skip_ref,
    xbuf,
    bcbuf,
    gbuf,
    ldc,
    dtc,
    start_ref,
    tot_ref,
    xs_ref,
    bcs_ref,
    y_ref,
    gain_ref,
    u_ref,
    brow_ref,
    acol_ref,
    sg_ref,
    colb_ref,
    drow_ref,
    grow_ref,
    ohe_ref,
    oht_ref,
    ohw_ref,
    tri_ref,
    st_ref,
    shift_ref,
    into_ref,
    intob_ref,
    dec_all,
    send1,
    recv1,
    send2,
    recv2,
    ss_all,
    in_sem,
    small_sem,
    halo_send,
    halo_recv,
    dec_send,
    dec_recv,
    one_send,
    one_recv,
    two_send,
    two_recv,
    ss_send,
    ss_recv,
):
    heads = ld_ref.shape[0]
    rows, width = out_ref.shape
    nc = rows // Q
    half = width // 2
    per = PIECES // nseq
    lanes = width // 128
    groups = ((0, nc // 5 * 2), (nc // 5 * 2, nc // 5 * 4), (nc // 5 * 4, nc))
    inner = width * nhead
    me = lax.axis_index("seq")
    mz = lax.axis_index("head")

    def seq_peer(i):
        return lax.rem(me + i, nseq)

    def head_peer(i):
        return lax.rem(mz + i, nhead)

    piece = rows // IN_PIECES
    blocks = nc // IN_PIECES

    def in_copies(k):
        at = pl.ds(pl.multiple_of(k * piece, piece), piece)
        to = pl.ds(pl.multiple_of(k * piece + HALO, HALO), piece)
        return (
            pltpu.make_async_copy(x_hbm.at[at], xbuf.at[to], in_sem.at[0, k]),
            pltpu.make_async_copy(bc_hbm.at[at], bcbuf.at[to], in_sem.at[1, k]),
        )

    gate_copy = pltpu.make_async_copy(gate_hbm, gbuf, in_sem.at[2, 0])

    small = [
        pltpu.make_async_copy(source, target, small_sem.at[k])
        for k, (source, target) in enumerate(
            [(ld_hbm, ld_ref), (dt_hbm, dt_ref), (kx_hbm, kx_ref), (kbc_hbm, kbc_ref), (skip_hbm, skip_ref), (gain_hbm, gain_ref)]
        )
    ]
    for copy in small:
        copy.start()
    for k in reversed(range(IN_PIECES)):
        for copy in in_copies(k):
            copy.start()

    barrier = pltpu.get_barrier_semaphore()

    def greet_seq(i, _):
        pl.semaphore_signal(barrier, inc=1, device_id={"seq": seq_peer(i)}, device_id_type=MESH)
        return 0

    def greet_head(i, _):
        pl.semaphore_signal(barrier, inc=1, device_id={"head": head_peer(i)}, device_id_type=MESH)
        return 0

    lax.fori_loop(1, nseq, greet_seq, 0)
    lax.fori_loop(1, nhead, greet_head, 0)

    gate_copy.start()

    def onehot(shape, picks):
        r = lax.broadcasted_iota(jnp.int32, shape, 0)
        h = lax.broadcasted_iota(jnp.int32, shape, 1) // HP
        hit = r == h + picks[0]
        for p in picks[1:]:
            hit = hit | (r == h + p)
        return jnp.where(hit, 1.0, 0.0)

    ohe_ref[...] = onehot((128, width), (16, 80)).astype(BF16)
    oht_ref[...] = onehot((128, width), (32, 96)).astype(BF16)
    ohw_ref[...] = onehot((128, width), (48, 64)).astype(BF16)
    row = lax.broadcasted_iota(jnp.int32, (Q, Q), 0)
    col = lax.broadcasted_iota(jnp.int32, (Q, Q), 1)
    tri_ref[...] = jnp.where(row <= col, 1.0, 0.0)
    tops = lax.broadcasted_iota(jnp.int32, (24, 24), 0)
    rests = lax.broadcasted_iota(jnp.int32, (24, 24), 1)
    later = jnp.where((rests > tops) & (rests < nc), 1.0, 0.0)
    ldc[...] = jnp.zeros_like(ldc)
    dtc[...] = jnp.ones_like(dtc)
    tot_ref[...] = jnp.zeros_like(tot_ref)
    for copy in small:
        copy.wait()
    for c in range(nc):
        at = slice(c * Q, c * Q + Q)
        ldc[16 * c : 16 * c + heads, :] = ld_ref[:, at]
        dtc[16 * c : 16 * c + heads, :] = dt_ref[:, at]

    tri = tri_ref[...].astype(BF16)
    cum = dot(jnp.concatenate(thirds(ldc[...]), axis=1), jnp.concatenate([tri, tri, tri], axis=0))
    step = dtc[...]
    tot = cum[:, Q - 1 : Q]
    brow_ref[...] = (cum - jnp.log(step)) * LOG2E
    ldc[...] = cum * LOG2E
    from_start = jnp.exp(cum)
    to_end = jnp.exp(tot - cum) * step
    start_ref[...] = from_start
    dtc[...] = to_end

    def turn(c, base):
        at = pl.ds(pl.multiple_of(16 * c, 16), 16)
        first, last = start_ref[at, :], dtc[at, :]
        first_hi = first.astype(BF16).astype(F32)
        last_hi = last.astype(BF16).astype(F32)
        power = ldc[at, :]
        whole = jnp.exp2(power + base)
        whole_hi = whole.astype(BF16).astype(F32)
        stack = jnp.concatenate(
            [
                power, first_hi, last_hi, whole_hi, whole - whole_hi, first - first_hi, last - last_hi,
                jnp.zeros((16, Q), F32),
            ],
            axis=0,
        ).T
        acol_ref[c] = stack
        colb_ref[c] = stack.astype(BF16)
        tot_ref[pl.ds(c, 1), :] = stack[Q - 1 : Q, :]
        return base + power[:, Q - 1 : Q]

    lax.fori_loop(0, nc, turn, jnp.zeros((16, 1), F32), unroll=5)

    heads_only = lax.broadcasted_iota(jnp.int32, (24, 128), 1) < 16
    totals = jnp.where(heads_only, tot_ref[...], 0.0)
    exponents = jnp.concatenate(
        [
            totals,
            dot(later, totals, precision=lax.Precision.HIGHEST),
            jnp.sum(totals, axis=0, keepdims=True) + jnp.zeros((16, 128), F32),
        ],
        axis=0,
    )
    factors = dot(
        jnp.concatenate([part[:, 0:32] for part in thirds(jnp.exp2(exponents))], axis=1),
        onehot((96, width), (0, 32, 64)).astype(BF16),
    )
    drow_ref[...] = factors[0:24]
    grow_ref[...] = factors[24:48]
    dec_all[me] = factors[48:49]
    st_ref[...] = jnp.zeros_like(st_ref)

    def halo_copies():
        peer = {"seq": seq_peer(1)}
        tail = pl.ds(rows, HALO)
        return (
            pltpu.make_async_remote_copy(
                xbuf.at[tail], xbuf.at[pl.ds(0, HALO)], halo_send.at[0], halo_recv.at[0],
                device_id=peer, device_id_type=MESH,
            ),
            pltpu.make_async_remote_copy(
                bcbuf.at[tail], bcbuf.at[pl.ds(0, HALO)], halo_send.at[1], halo_recv.at[1],
                device_id=peer, device_id_type=MESH,
            ),
        )

    def dec_copy(peer, source):
        return pltpu.make_async_remote_copy(
            dec_all.at[source], dec_all.at[source], dec_send.at[peer], dec_recv.at[source],
            device_id={"seq": peer}, device_id_type=MESH,
        )

    def phase_a(c, side):
        window = pl.ds(pl.multiple_of(c * Q, Q), Q + HALO)
        stack = colb_ref[c]
        grow = grow_ref[pl.ds(c, 1), :]
        taps = kbc_ref[...].astype(F32) * 0.5
        bcs = [
            conv_half_silu(
                bcbuf[window, 128 * j : 128 * j + 128], taps[:, 128 * j : 128 * j + 128],
                shift_ref.at[side, lanes + j],
            ).astype(BF16)
            for j in range(1)
        ]
        bcs_ref[c, :, 0:128] = bcs[0]
        taps = kx_ref[...].astype(F32) * 0.5
        for j in range(0, lanes, 2):
            wide = slice(128 * j, 128 * j + 256)
            ends = dot(stack, oht_ref[:, wide])
            weighted = []
            for t in range(2):
                cols = slice(128 * (j + t), 128 * (j + t) + 128)
                xs = conv_half_silu(xbuf[window, cols], taps[:, cols], shift_ref.at[side, j + t])
                xs_ref[c, :, cols] = xs.astype(BF16)
                weighted.append((xs * ends[:, 128 * t : 128 * t + 128]).astype(BF16))
            update = dot(bcs[0], jnp.concatenate(weighted, axis=1), 0, 0)
            u_ref[c, :, wide] = update
            st_ref[:, wide] += grow[:, wide] * update

    def piece_a(i, _):
        k = IN_PIECES - 1 - i

        @pl.when(k > 0)
        def _():
            for copy in in_copies(k - 1):
                copy.wait()

        @pl.when(i == GREET_PIECE)
        def _():
            pl.semaphore_wait(barrier, nseq - 1 + nhead - 1)
            for copy in halo_copies():
                copy.start()

            def send(k, _):
                dec_copy(seq_peer(k), me).start()
                return 0

            lax.fori_loop(1, nseq, send, 0)

        @pl.when(k == 0)
        def _():
            for copy in halo_copies():
                copy.wait_recv()

            @pl.when(me == 0)
            def _():
                xbuf[0:HALO, :] = jnp.zeros((HALO, width), BF16)
                bcbuf[0:HALO, :] = jnp.zeros((HALO, 2 * NS), BF16)

        def block(b, _):
            for side in range(2):
                phase_a(k * blocks + blocks - 1 - 2 * b - side, side)
            return 0

        lax.fori_loop(0, blocks // 2, block, 0)
        return 0

    for copy in in_copies(IN_PIECES - 1):
        copy.wait()
    lax.fori_loop(0, IN_PIECES, piece_a, 0)

    for q in range(PIECES):
        r, l = q // 2, q % 2
        send1[q // per, q % per] = st_ref[8 * r : 8 * r + 8, half * l : half * l + half].astype(BF16)
    recv1[me] = send1[me]

    def one_copy(peer, source):
        return pltpu.make_async_remote_copy(
            send1.at[peer], recv1.at[source], one_send.at[peer], one_recv.at[source],
            device_id={"seq": peer}, device_id_type=MESH,
        )

    def two_copy(peer, source):
        return pltpu.make_async_remote_copy(
            send2.at[peer], recv2.at[source], two_send.at[peer], two_recv.at[source],
            device_id={"seq": peer}, device_id_type=MESH,
        )

    def send_one(k, _):
        one_copy(seq_peer(k), me).start()
        return 0

    lax.fori_loop(1, nseq, send_one, 0, unroll=True)

    def second_round():
        def arrived(k, _):
            peer = seq_peer(k)
            dec_copy(peer, peer).wait_recv()
            one_copy(peer, peer).wait_recv()
            return 0

        lax.fori_loop(1, nseq, arrived, 0)
        for e in range(per):
            l = lax.rem(me * per + e, 2)
            cols = pl.ds(pl.multiple_of(l * half, 128), half)

            def scan(k, acc):
                send2[k, e] = acc.astype(BF16)
                return dec_all[k, :, cols] * acc + recv1[k, e].astype(F32)

            lax.fori_loop(0, nseq, scan, jnp.zeros((8, half), F32), unroll=8)
        recv2[me] = send2[me]

        def send_two(k, _):
            two_copy(seq_peer(k), me).start()
            return 0

        lax.fori_loop(1, nseq, send_two, 0, unroll=True)

    lane = lax.broadcasted_iota(jnp.int32, (Q, 128), 1)
    left = jnp.where(lane < HP, 1.0, 0.0).astype(BF16)
    right = jnp.where(lane < HP, 0.0, 1.0).astype(BF16)
    first_head = lax.broadcasted_iota(jnp.int32, (1, 128), 1) < HP
    lower = lax.broadcasted_iota(jnp.int32, (Q, Q), 0) >= lax.broadcasted_iota(jnp.int32, (Q, Q), 1)

    def phase_b(i, _):
        both = pl.ds(2 * i, 2)
        all_columns = colb_ref[both].reshape(2 * Q, 128)
        scores, drow = [], []
        for t in range(2):
            c = 2 * i + t
            bcs_ref[c, :, 128:256] = conv_half_silu(
                bcbuf[pl.ds(pl.multiple_of(c * Q, Q), Q + HALO), 128:256],
                kbc_ref[:, 128:256].astype(F32) * 0.5,
                shift_ref.at[t, lanes + 1],
            ).astype(BF16)
            scores.append(
                jnp.where(lower, dot(bcs_ref[c, :, 128:256], bcs_ref[c, :, 0:128], 1, 1), 0.0)
            )
            drow.append(drow_ref[pl.ds(c, 1), :])
        for j in range(0, lanes, 2):
            wide = slice(128 * j, 128 * j + 256)
            decays = dot(all_columns, ohe_ref[:, wide])
            for t in range(2):
                c = 2 * i + t
                at = pl.ds(pl.multiple_of(c * Q, Q), Q)
                state = st_ref[:, wide]
                st_ref[:, wide] = drow[t][:, wide] * state + u_ref[c, :, wide]
                carried = dot(bcs_ref[c, :, 128:256], state.astype(BF16)) * decays[Q * t : Q * t + Q]
                for k in range(2):
                    cols = slice(128 * (j + k), 128 * (j + k) + 128)
                    weights = []
                    for h in (2 * (j + k), 2 * (j + k) + 1):
                        gap = acol_ref[c, :, h : h + 1] - brow_ref[pl.ds(16 * c + h, 1), :]
                        weights.append((scores[t] * jnp.exp2(jnp.minimum(gap, 0.0))).astype(BF16))
                    xs = xs_ref[c, :, cols]
                    pair = jnp.concatenate([xs * left, xs * right], axis=0)
                    intra = dot(jnp.concatenate(weights, axis=1), pair)
                    skip = jnp.where(first_head, skip_ref[2 * (j + k)], skip_ref[2 * (j + k) + 1])
                    y_ref[c, :, cols] = intra + skip * xs.astype(F32) + carried[:, 128 * k : 128 * k + 128]
                    h = gbuf[at, cols].astype(F32) * 0.5
                    sg_ref[c, :, cols] = h + h * jnp.tanh(h)
        return 0

    gate_copy.wait()
    st_ref[...] = jnp.zeros_like(st_ref)
    split = nc // 4
    lax.fori_loop(0, split, phase_b, 0)
    second_round()
    lax.fori_loop(split, nc // 2, phase_b, 0)

    def arrived_two(k, _):
        peer = seq_peer(k)
        two_copy(peer, peer).wait_recv()
        return 0

    lax.fori_loop(1, nseq, arrived_two, 0)
    for q in range(PIECES):
        r, l = q // 2, q % 2
        into_ref[8 * r : 8 * r + 8, half * l : half * l + half] = recv2[q // per, q % per].astype(F32)
    intob_ref[...] = into_ref[...].astype(BF16)

    def ss_copy(peer, source, g):
        part = pl.ds(groups[g][0], groups[g][1] - groups[g][0])
        return pltpu.make_async_remote_copy(
            ss_all.at[source, part], ss_all.at[source, part],
            ss_send.at[peer, g], ss_recv.at[source, g],
            device_id={"head": peer}, device_id_type=MESH,
        )

    def phase_c(i, _):
        both = pl.ds(2 * i, 2)
        cs = bcs_ref[both, :, 128:256].reshape(2 * Q, 128)
        columns = colb_ref[both].reshape(2 * Q, 128)
        ss = None
        for j in range(0, lanes, 2):
            wide = slice(128 * j, 128 * j + 256)
            carried = dot(cs, intob_ref[:, wide]) * dot(columns, ohw_ref[:, wide])
            mixed = y_ref[both, :, wide].reshape(2 * Q, 256) + carried
            gated = mixed * sg_ref[both, :, wide].reshape(2 * Q, 256)
            u_ref[both, :, wide] = gated.reshape(2, Q, 256)
            square = gated * gated
            part = square[:, :128] + square[:, 128:]
            ss = part if ss is None else ss + part
        ss = ss.astype(BF16)
        for t in range(2):
            ss_all[mz, 2 * i + t] = dot(jnp.ones((8, 128), BF16), ss[Q * t : Q * t + Q], 1, 1)[0:1]
        return 0

    for g in range(len(groups)):
        lax.fori_loop(groups[g][0] // 2, groups[g][1] // 2, phase_c, 0)

        def send_ss(k, _):
            ss_copy(head_peer(k), mz, g).start()
            return 0

        lax.fori_loop(1, nhead, send_ss, 0, unroll=True)

    eye = lax.broadcasted_iota(jnp.int32, (Q, Q), 0) == lax.broadcasted_iota(jnp.int32, (Q, Q), 1)
    gain = gain_ref[...].reshape(1, width)

    def phase_d(c, _):
        square = ss_all[0, c]
        for p in range(1, nhead):
            square = square + ss_all[p, c]
        scale = lax.rsqrt(square * (1.0 / inner) + 1e-05)
        scale = jnp.sum(jnp.where(eye, scale, 0.0), axis=1, keepdims=True)
        at = pl.ds(pl.multiple_of(c * Q, Q), Q)
        for j in range(lanes):
            cols = slice(128 * j, 128 * j + 128)
            out_ref[at, cols] = (u_ref[c, :, cols] * scale * gain[:, cols]).astype(BF16)
        return 0

    for copy in halo_copies():
        copy.wait_send()

    def left_seq(k, _):
        peer = seq_peer(k)
        dec_copy(peer, me).wait_send()
        one_copy(peer, me).wait_send()
        two_copy(peer, me).wait_send()
        return 0

    lax.fori_loop(1, nseq, left_seq, 0)

    for g in range(len(groups)):

        def arrived_ss(k, _):
            peer = head_peer(k)
            ss_copy(peer, peer, g).wait_recv()
            return 0

        lax.fori_loop(1, nhead, arrived_ss, 0)
        lax.fori_loop(*groups[g], phase_d, 0, unroll=2)

    def left_head(k, _):
        for g in range(len(groups)):
            ss_copy(head_peer(k), mz, g).wait_send()
        return 0

    lax.fori_loop(1, nhead, left_head, 0)


def per_device(nseq, nhead, x_in, bc_in, gate_in, log_decay, step_size, conv_x, conv_bc, skip_gain, norm_gain):
    rows, width = x_in.shape
    heads = log_decay.shape[0]
    nc = rows // Q
    per = PIECES // nseq
    half = width // 2
    groups = 3
    vmem = pl.BlockSpec(memory_space=pltpu.VMEM)
    dma = pltpu.SemaphoreType.DMA
    return pl.pallas_call(
        functools.partial(kernel, nseq, nhead),
        out_shape=pltpu.VMEM((rows, width), BF16),
        in_specs=[pl.BlockSpec(memory_space=pltpu.HBM)] * 9,
        out_specs=vmem,
        scratch_shapes=[
            pltpu.VMEM((heads, rows), F32),
            pltpu.VMEM((heads, rows), F32),
            pltpu.VMEM((CONV, width), BF16),
            pltpu.VMEM((CONV, 2 * NS), BF16),
            pltpu.SMEM((heads,), F32),
            pltpu.VMEM((HALO + rows, width), BF16),
            pltpu.VMEM((HALO + rows, 2 * NS), BF16),
            pltpu.VMEM((rows, width), BF16),
            pltpu.VMEM((16 * nc, Q), F32),
            pltpu.VMEM((16 * nc, Q), F32),
            pltpu.VMEM((16 * nc, Q), F32),
            pltpu.VMEM((24, 128), F32),
            pltpu.VMEM((nc, Q, width), BF16),
            pltpu.VMEM((nc, Q, 2 * NS), BF16),
            pltpu.VMEM((nc, Q, width), F32),
            pltpu.VMEM((width,), F32),
            pltpu.VMEM((nc, NS, width), F32),
            pltpu.VMEM((16 * nc, Q), F32),
            pltpu.VMEM((nc, Q, 128), F32),
            pltpu.VMEM((nc, Q, width), F32),
            pltpu.VMEM((nc, Q, 128), BF16),
            pltpu.VMEM((24, width), F32),
            pltpu.VMEM((24, width), F32),
            pltpu.VMEM((128, width), BF16),
            pltpu.VMEM((128, width), BF16),
            pltpu.VMEM((128, width), BF16),
            pltpu.VMEM((Q, Q), F32),
            pltpu.VMEM((NS, width), F32),
            pltpu.VMEM((2, width // 128 + 2, Q + 8, 128), F32),
            pltpu.VMEM((NS, width), F32),
            pltpu.VMEM((NS, width), BF16),
            pltpu.VMEM((nseq, 1, width), F32),
            pltpu.VMEM((nseq, per, 8, half), BF16),
            pltpu.VMEM((nseq, per, 8, half), BF16),
            pltpu.VMEM((nseq, per, 8, half), BF16),
            pltpu.VMEM((nseq, per, 8, half), BF16),
            pltpu.VMEM((nhead, nc, 1, Q), F32),
            dma((3, IN_PIECES)),
            dma((6,)),
            dma((2,)), dma((2,)),
            dma((nseq,)), dma((nseq,)),
            dma((nseq,)), dma((nseq,)),
            dma((nseq,)), dma((nseq,)),
            dma((nhead, groups)), dma((nhead, groups)),
        ],
        compiler_params=pltpu.CompilerParams(
            collective_id=0, has_side_effects=True, vmem_limit_bytes=VMEM_LIMIT
        ),
        name="mamba",
    )(
        *(
            pltpu.with_memory_space_constraint(a, pltpu.HBM)
            for a in (x_in, bc_in, gate_in, log_decay, step_size, conv_x, conv_bc, skip_gain, norm_gain)
        )
    )


def solution(mesh):
    in_specs = (
        P("seq", "head"),
        P("seq", None),
        P("seq", "head"),
        P("head", "seq"),
        P("head", "seq"),
        P(None, "head"),
        P(),
        P("head"),
        P("head"),
    )
    return jax.shard_map(
        functools.partial(per_device, mesh.shape["seq"], mesh.shape["head"]),
        mesh=mesh,
        in_specs=in_specs,
        out_specs=P("seq", "head"),
        check_vma=False,
    )
```

```python
import functools

import jax
import jax.numpy as jnp
from jax import lax
from jax.experimental import pallas as pl
from jax.experimental.pallas import tpu as pltpu
from jax.sharding import PartitionSpec as P

HP = 64
NS = 128
CONV = 4
Q = 128
HALO = 16
PIECES = 32
IN_PIECES = 5
GREET_PIECE = 1
VMEM_LIMIT = 56 * 1024 * 1024
LOG2E = 1.4426950408889634
F32 = jnp.float32
BF16 = jnp.bfloat16
MESH = pl.DeviceIdType.MESH


def dot(a, b, ca=1, cb=0, precision=None):
    return lax.dot_general(
        a, b, (((ca,), (cb,)), ((), ())), preferred_element_type=F32, precision=precision
    )


def thirds(a):
    hi = a.astype(BF16)
    rest = a - hi.astype(F32)
    mid = rest.astype(BF16)
    return hi, mid, (rest - mid.astype(F32)).astype(BF16)


def conv_half_silu(window, taps, shift):
    shift[...] = window[HALO - 8 :].astype(F32)
    h = None
    for o in range(CONV):
        start = 8 - (CONV - 1) + o
        term = shift[start : start + Q] * taps[o : o + 1]
        h = term if h is None else h + term
    return h + h * jnp.tanh(h)


def kernel(
    nseq,
    nhead,
    x_hbm,
    bc_hbm,
    gate_hbm,
    ld_hbm,
    dt_hbm,
    kx_hbm,
    kbc_hbm,
    skip_hbm,
    gain_hbm,
    out_ref,
    ld_ref,
    dt_ref,
    kx_ref,
    kbc_ref,
    skip_ref,
    xbuf,
    bcbuf,
    gbuf,
    ldc,
    dtc,
    start_ref,
    tot_ref,
    xs_ref,
    bcs_ref,
    y_ref,
    gain_ref,
    u_ref,
    brow_ref,
    acol_ref,
    sg_ref,
    colb_ref,
    drow_ref,
    grow_ref,
    ohe_ref,
    oht_ref,
    ohw_ref,
    tri_ref,
    st_ref,
    shift_ref,
    into_ref,
    intob_ref,
    dec_all,
    send1,
    recv1,
    send2,
    recv2,
    ss_all,
    in_sem,
    small_sem,
    halo_send,
    halo_recv,
    dec_send,
    dec_recv,
    one_send,
    one_recv,
    two_send,
    two_recv,
    ss_send,
    ss_recv,
):
    heads = ld_ref.shape[0]
    rows, width = out_ref.shape
    nc = rows // Q
    half = width // 2
    per = PIECES // nseq
    lanes = width // 128
    groups = ((0, nc // 5 * 2), (nc // 5 * 2, nc // 5 * 4), (nc // 5 * 4, nc))
    inner = width * nhead
    me = lax.axis_index("seq")
    mz = lax.axis_index("head")

    def seq_peer(i):
        return lax.rem(me + i, nseq)

    def head_peer(i):
        return lax.rem(mz + i, nhead)

    piece = rows // IN_PIECES
    blocks = nc // IN_PIECES

    def in_copies(k):
        at = pl.ds(pl.multiple_of(k * piece, piece), piece)
        to = pl.ds(pl.multiple_of(k * piece + HALO, HALO), piece)
        return (
            pltpu.make_async_copy(x_hbm.at[at], xbuf.at[to], in_sem.at[0, k]),
            pltpu.make_async_copy(bc_hbm.at[at], bcbuf.at[to], in_sem.at[1, k]),
        )

    gate_copy = pltpu.make_async_copy(gate_hbm, gbuf, in_sem.at[2, 0])

    small = [
        pltpu.make_async_copy(source, target, small_sem.at[k])
        for k, (source, target) in enumerate(
            [(ld_hbm, ld_ref), (dt_hbm, dt_ref), (kx_hbm, kx_ref), (kbc_hbm, kbc_ref), (skip_hbm, skip_ref), (gain_hbm, gain_ref)]
        )
    ]
    for copy in small:
        copy.start()
    for k in reversed(range(IN_PIECES)):
        for copy in in_copies(k):
            copy.start()

    barrier = pltpu.get_barrier_semaphore()

    def greet_seq(i, _):
        pl.semaphore_signal(barrier, inc=1, device_id={"seq": seq_peer(i)}, device_id_type=MESH)
        return 0

    def greet_head(i, _):
        pl.semaphore_signal(barrier, inc=1, device_id={"head": head_peer(i)}, device_id_type=MESH)
        return 0

    lax.fori_loop(1, nseq, greet_seq, 0)
    lax.fori_loop(1, nhead, greet_head, 0)

    gate_copy.start()

    def onehot(shape, picks):
        r = lax.broadcasted_iota(jnp.int32, shape, 0)
        h = lax.broadcasted_iota(jnp.int32, shape, 1) // HP
        hit = r == h + picks[0]
        for p in picks[1:]:
            hit = hit | (r == h + p)
        return jnp.where(hit, 1.0, 0.0)

    ohe_ref[...] = onehot((128, width), (16, 80)).astype(BF16)
    oht_ref[...] = onehot((128, width), (32, 96)).astype(BF16)
    ohw_ref[...] = onehot((128, width), (48, 64)).astype(BF16)
    row = lax.broadcasted_iota(jnp.int32, (Q, Q), 0)
    col = lax.broadcasted_iota(jnp.int32, (Q, Q), 1)
    tri_ref[...] = jnp.where(row <= col, 1.0, 0.0)
    tops = lax.broadcasted_iota(jnp.int32, (24, 24), 0)
    rests = lax.broadcasted_iota(jnp.int32, (24, 24), 1)
    later = jnp.where((rests > tops) & (rests < nc), 1.0, 0.0)
    ldc[...] = jnp.zeros_like(ldc)
    dtc[...] = jnp.ones_like(dtc)
    tot_ref[...] = jnp.zeros_like(tot_ref)
    for copy in small:
        copy.wait()
    for c in range(nc):
        at = slice(c * Q, c * Q + Q)
        ldc[16 * c : 16 * c + heads, :] = ld_ref[:, at]
        dtc[16 * c : 16 * c + heads, :] = dt_ref[:, at]

    tri = tri_ref[...].astype(BF16)
    cum = dot(jnp.concatenate(thirds(ldc[...]), axis=1), jnp.concatenate([tri, tri, tri], axis=0))
    step = dtc[...]
    tot = cum[:, Q - 1 : Q]
    brow_ref[...] = (cum - jnp.log(step)) * LOG2E
    ldc[...] = cum * LOG2E
    from_start = jnp.exp(cum)
    to_end = jnp.exp(tot - cum) * step
    start_ref[...] = from_start
    dtc[...] = to_end

    def turn(c, base):
        at = pl.ds(pl.multiple_of(16 * c, 16), 16)
        first, last = start_ref[at, :], dtc[at, :]
        first_hi = first.astype(BF16).astype(F32)
        last_hi = last.astype(BF16).astype(F32)
        power = ldc[at, :]
        whole = jnp.exp2(power + base)
        whole_hi = whole.astype(BF16).astype(F32)
        stack = jnp.concatenate(
            [
                power, first_hi, last_hi, whole_hi, whole - whole_hi, first - first_hi, last - last_hi,
                jnp.zeros((16, Q), F32),
            ],
            axis=0,
        ).T
        acol_ref[c] = stack
        colb_ref[c] = stack.astype(BF16)
        tot_ref[pl.ds(c, 1), :] = stack[Q - 1 : Q, :]
        return base + power[:, Q - 1 : Q]

    lax.fori_loop(0, nc, turn, jnp.zeros((16, 1), F32), unroll=5)

    heads_only = lax.broadcasted_iota(jnp.int32, (24, 128), 1) < 16
    totals = jnp.where(heads_only, tot_ref[...], 0.0)
    exponents = jnp.concatenate(
        [
            totals,
            dot(later, totals, precision=lax.Precision.HIGHEST),
            jnp.sum(totals, axis=0, keepdims=True) + jnp.zeros((16, 128), F32),
        ],
        axis=0,
    )
    factors = dot(
        jnp.concatenate([part[:, 0:32] for part in thirds(jnp.exp2(exponents))], axis=1),
        onehot((96, width), (0, 32, 64)).astype(BF16),
    )
    drow_ref[...] = factors[0:24]
    grow_ref[...] = factors[24:48]
    dec_all[me] = factors[48:49]
    st_ref[...] = jnp.zeros_like(st_ref)

    def halo_copies():
        peer = {"seq": seq_peer(1)}
        tail = pl.ds(rows, HALO)
        return (
            pltpu.make_async_remote_copy(
                xbuf.at[tail], xbuf.at[pl.ds(0, HALO)], halo_send.at[0], halo_recv.at[0],
                device_id=peer, device_id_type=MESH,
            ),
            pltpu.make_async_remote_copy(
                bcbuf.at[tail], bcbuf.at[pl.ds(0, HALO)], halo_send.at[1], halo_recv.at[1],
                device_id=peer, device_id_type=MESH,
            ),
        )

    def dec_copy(peer, source):
        return pltpu.make_async_remote_copy(
            dec_all.at[source], dec_all.at[source], dec_send.at[peer], dec_recv.at[source],
            device_id={"seq": peer}, device_id_type=MESH,
        )

    def phase_a(c, side):
        window = pl.ds(pl.multiple_of(c * Q, Q), Q + HALO)
        stack = colb_ref[c]
        grow = grow_ref[pl.ds(c, 1), :]
        taps = kbc_ref[...].astype(F32) * 0.5
        bcs = [
            conv_half_silu(
                bcbuf[window, 128 * j : 128 * j + 128], taps[:, 128 * j : 128 * j + 128],
                shift_ref.at[side, lanes + j],
            ).astype(BF16)
            for j in range(1)
        ]
        bcs_ref[c, :, 0:128] = bcs[0]
        taps = kx_ref[...].astype(F32) * 0.5
        for j in range(0, lanes, 2):
            wide = slice(128 * j, 128 * j + 256)
            ends = dot(stack, oht_ref[:, wide])
            weighted = []
            for t in range(2):
                cols = slice(128 * (j + t), 128 * (j + t) + 128)
                xs = conv_half_silu(xbuf[window, cols], taps[:, cols], shift_ref.at[side, j + t])
                xs_ref[c, :, cols] = xs.astype(BF16)
                weighted.append((xs * ends[:, 128 * t : 128 * t + 128]).astype(BF16))
            update = dot(bcs[0], jnp.concatenate(weighted, axis=1), 0, 0)
            u_ref[c, :, wide] = update
            st_ref[:, wide] += grow[:, wide] * update

    def piece_a(i, _):
        k = IN_PIECES - 1 - i

        @pl.when(k > 0)
        def _():
            for copy in in_copies(k - 1):
                copy.wait()

        @pl.when(i == GREET_PIECE)
        def _():
            pl.semaphore_wait(barrier, nseq - 1 + nhead - 1)
            for copy in halo_copies():
                copy.start()

            def send(k, _):
                dec_copy(seq_peer(k), me).start()
                return 0

            lax.fori_loop(1, nseq, send, 0)

        @pl.when(k == 0)
        def _():
            for copy in halo_copies():
                copy.wait_recv()

            @pl.when(me == 0)
            def _():
                xbuf[0:HALO, :] = jnp.zeros((HALO, width), BF16)
                bcbuf[0:HALO, :] = jnp.zeros((HALO, 2 * NS), BF16)

        def block(b, _):
            for side in range(2):
                phase_a(k * blocks + blocks - 1 - 2 * b - side, side)
            return 0

        lax.fori_loop(0, blocks // 2, block, 0)
        return 0

    for copy in in_copies(IN_PIECES - 1):
        copy.wait()
    lax.fori_loop(0, IN_PIECES, piece_a, 0)

    for q in range(PIECES):
        r, l = q // 2, q % 2
        send1[q // per, q % per] = st_ref[8 * r : 8 * r + 8, half * l : half * l + half].astype(BF16)
    recv1[me] = send1[me]

    def one_copy(peer, source):
        return pltpu.make_async_remote_copy(
            send1.at[peer], recv1.at[source], one_send.at[peer], one_recv.at[source],
            device_id={"seq": peer}, device_id_type=MESH,
        )

    def two_copy(peer, source):
        return pltpu.make_async_remote_copy(
            send2.at[peer], recv2.at[source], two_send.at[peer], two_recv.at[source],
            device_id={"seq": peer}, device_id_type=MESH,
        )

    def send_one(k, _):
        one_copy(seq_peer(lax.rem(k + nseq // 4, nseq - 1) + 1), me).start()
        return 0

    lax.fori_loop(1, nseq, send_one, 0, unroll=True)

    def second_round():
        def arrived(k, _):
            peer = seq_peer(k)
            dec_copy(peer, peer).wait_recv()
            one_copy(peer, peer).wait_recv()
            return 0

        lax.fori_loop(1, nseq, arrived, 0)
        for e in range(per):
            l = lax.rem(me * per + e, 2)
            cols = pl.ds(pl.multiple_of(l * half, 128), half)

            def scan(k, acc):
                send2[k, e] = acc.astype(BF16)
                return dec_all[k, :, cols] * acc + recv1[k, e].astype(F32)

            lax.fori_loop(0, nseq, scan, jnp.zeros((8, half), F32), unroll=8)
        recv2[me] = send2[me]

        def send_two(k, _):
            two_copy(seq_peer(lax.rem(k + nseq // 4, nseq - 1) + 1), me).start()
            return 0

        lax.fori_loop(1, nseq, send_two, 0, unroll=True)

    lane = lax.broadcasted_iota(jnp.int32, (Q, 128), 1)
    left = jnp.where(lane < HP, 1.0, 0.0).astype(BF16)
    right = jnp.where(lane < HP, 0.0, 1.0).astype(BF16)
    first_head = lax.broadcasted_iota(jnp.int32, (1, 128), 1) < HP
    lower = lax.broadcasted_iota(jnp.int32, (Q, Q), 0) >= lax.broadcasted_iota(jnp.int32, (Q, Q), 1)

    def phase_b(i, _):
        both = pl.ds(2 * i, 2)
        all_columns = colb_ref[both].reshape(2 * Q, 128)
        scores, drow = [], []
        for t in range(2):
            c = 2 * i + t
            bcs_ref[c, :, 128:256] = conv_half_silu(
                bcbuf[pl.ds(pl.multiple_of(c * Q, Q), Q + HALO), 128:256],
                kbc_ref[:, 128:256].astype(F32) * 0.5,
                shift_ref.at[t, lanes + 1],
            ).astype(BF16)
            scores.append(
                jnp.where(lower, dot(bcs_ref[c, :, 128:256], bcs_ref[c, :, 0:128], 1, 1), 0.0)
            )
            drow.append(drow_ref[pl.ds(c, 1), :])
        for j in range(0, lanes, 2):
            wide = slice(128 * j, 128 * j + 256)
            decays = dot(all_columns, ohe_ref[:, wide])
            for t in range(2):
                c = 2 * i + t
                at = pl.ds(pl.multiple_of(c * Q, Q), Q)
                state = st_ref[:, wide]
                st_ref[:, wide] = drow[t][:, wide] * state + u_ref[c, :, wide]
                carried = dot(bcs_ref[c, :, 128:256], state.astype(BF16)) * decays[Q * t : Q * t + Q]
                for k in range(2):
                    cols = slice(128 * (j + k), 128 * (j + k) + 128)
                    weights = []
                    for h in (2 * (j + k), 2 * (j + k) + 1):
                        gap = acol_ref[c, :, h : h + 1] - brow_ref[pl.ds(16 * c + h, 1), :]
                        weights.append((scores[t] * jnp.exp2(jnp.minimum(gap, 0.0))).astype(BF16))
                    xs = xs_ref[c, :, cols]
                    pair = jnp.concatenate([xs * left, xs * right], axis=0)
                    intra = dot(jnp.concatenate(weights, axis=1), pair)
                    skip = jnp.where(first_head, skip_ref[2 * (j + k)], skip_ref[2 * (j + k) + 1])
                    y_ref[c, :, cols] = intra + skip * xs.astype(F32) + carried[:, 128 * k : 128 * k + 128]
                    h = gbuf[at, cols].astype(F32) * 0.5
                    sg_ref[c, :, cols] = h + h * jnp.tanh(h)
        return 0

    gate_copy.wait()
    st_ref[...] = jnp.zeros_like(st_ref)
    split = nc // 4
    lax.fori_loop(0, split, phase_b, 0)
    second_round()
    lax.fori_loop(split, nc // 2, phase_b, 0)

    def arrived_two(k, _):
        peer = seq_peer(k)
        two_copy(peer, peer).wait_recv()
        return 0

    lax.fori_loop(1, nseq, arrived_two, 0)
    for q in range(PIECES):
        r, l = q // 2, q % 2
        into_ref[8 * r : 8 * r + 8, half * l : half * l + half] = recv2[q // per, q % per].astype(F32)
    intob_ref[...] = into_ref[...].astype(BF16)

    def ss_copy(peer, source, g):
        part = pl.ds(groups[g][0], groups[g][1] - groups[g][0])
        return pltpu.make_async_remote_copy(
            ss_all.at[source, part], ss_all.at[source, part],
            ss_send.at[peer, g], ss_recv.at[source, g],
            device_id={"head": peer}, device_id_type=MESH,
        )

    def phase_c(i, _):
        both = pl.ds(2 * i, 2)
        cs = bcs_ref[both, :, 128:256].reshape(2 * Q, 128)
        columns = colb_ref[both].reshape(2 * Q, 128)
        ss = None
        for j in range(0, lanes, 2):
            wide = slice(128 * j, 128 * j + 256)
            carried = dot(cs, intob_ref[:, wide]) * dot(columns, ohw_ref[:, wide])
            mixed = y_ref[both, :, wide].reshape(2 * Q, 256) + carried
            gated = mixed * sg_ref[both, :, wide].reshape(2 * Q, 256)
            u_ref[both, :, wide] = gated.reshape(2, Q, 256)
            square = gated * gated
            part = square[:, :128] + square[:, 128:]
            ss = part if ss is None else ss + part
        ss = ss.astype(BF16)
        for t in range(2):
            ss_all[mz, 2 * i + t] = dot(jnp.ones((8, 128), BF16), ss[Q * t : Q * t + Q], 1, 1)[0:1]
        return 0

    for g in range(len(groups)):
        lax.fori_loop(groups[g][0] // 2, groups[g][1] // 2, phase_c, 0)

        def send_ss(k, _):
            ss_copy(head_peer(k), mz, g).start()
            return 0

        lax.fori_loop(1, nhead, send_ss, 0, unroll=True)

    eye = lax.broadcasted_iota(jnp.int32, (Q, Q), 0) == lax.broadcasted_iota(jnp.int32, (Q, Q), 1)
    gain = gain_ref[...].reshape(1, width)

    def phase_d(c, _):
        square = ss_all[0, c]
        for p in range(1, nhead):
            square = square + ss_all[p, c]
        scale = lax.rsqrt(square * (1.0 / inner) + 1e-05)
        scale = jnp.sum(jnp.where(eye, scale, 0.0), axis=1, keepdims=True)
        at = pl.ds(pl.multiple_of(c * Q, Q), Q)
        for j in range(lanes):
            cols = slice(128 * j, 128 * j + 128)
            out_ref[at, cols] = (u_ref[c, :, cols] * scale * gain[:, cols]).astype(BF16)
        return 0

    for copy in halo_copies():
        copy.wait_send()

    def left_seq(k, _):
        peer = seq_peer(k)
        dec_copy(peer, me).wait_send()
        one_copy(peer, me).wait_send()
        two_copy(peer, me).wait_send()
        return 0

    lax.fori_loop(1, nseq, left_seq, 0)

    for g in range(len(groups)):

        def arrived_ss(k, _):
            peer = head_peer(k)
            ss_copy(peer, peer, g).wait_recv()
            return 0

        lax.fori_loop(1, nhead, arrived_ss, 0)
        lax.fori_loop(*groups[g], phase_d, 0, unroll=2)

    def left_head(k, _):
        for g in range(len(groups)):
            ss_copy(head_peer(k), mz, g).wait_send()
        return 0

    lax.fori_loop(1, nhead, left_head, 0)


def per_device(nseq, nhead, x_in, bc_in, gate_in, log_decay, step_size, conv_x, conv_bc, skip_gain, norm_gain):
    rows, width = x_in.shape
    heads = log_decay.shape[0]
    nc = rows // Q
    per = PIECES // nseq
    half = width // 2
    groups = 3
    vmem = pl.BlockSpec(memory_space=pltpu.VMEM)
    dma = pltpu.SemaphoreType.DMA
    return pl.pallas_call(
        functools.partial(kernel, nseq, nhead),
        out_shape=pltpu.VMEM((rows, width), BF16),
        in_specs=[pl.BlockSpec(memory_space=pltpu.HBM)] * 9,
        out_specs=vmem,
        scratch_shapes=[
            pltpu.VMEM((heads, rows), F32),
            pltpu.VMEM((heads, rows), F32),
            pltpu.VMEM((CONV, width), BF16),
            pltpu.VMEM((CONV, 2 * NS), BF16),
            pltpu.SMEM((heads,), F32),
            pltpu.VMEM((HALO + rows, width), BF16),
            pltpu.VMEM((HALO + rows, 2 * NS), BF16),
            pltpu.VMEM((rows, width), BF16),
            pltpu.VMEM((16 * nc, Q), F32),
            pltpu.VMEM((16 * nc, Q), F32),
            pltpu.VMEM((16 * nc, Q), F32),
            pltpu.VMEM((24, 128), F32),
            pltpu.VMEM((nc, Q, width), BF16),
            pltpu.VMEM((nc, Q, 2 * NS), BF16),
            pltpu.VMEM((nc, Q, width), F32),
            pltpu.VMEM((width,), F32),
            pltpu.VMEM((nc, NS, width), F32),
            pltpu.VMEM((16 * nc, Q), F32),
            pltpu.VMEM((nc, Q, 128), F32),
            pltpu.VMEM((nc, Q, width), F32),
            pltpu.VMEM((nc, Q, 128), BF16),
            pltpu.VMEM((24, width), F32),
            pltpu.VMEM((24, width), F32),
            pltpu.VMEM((128, width), BF16),
            pltpu.VMEM((128, width), BF16),
            pltpu.VMEM((128, width), BF16),
            pltpu.VMEM((Q, Q), F32),
            pltpu.VMEM((NS, width), F32),
            pltpu.VMEM((2, width // 128 + 2, Q + 8, 128), F32),
            pltpu.VMEM((NS, width), F32),
            pltpu.VMEM((NS, width), BF16),
            pltpu.VMEM((nseq, 1, width), F32),
            pltpu.VMEM((nseq, per, 8, half), BF16),
            pltpu.VMEM((nseq, per, 8, half), BF16),
            pltpu.VMEM((nseq, per, 8, half), BF16),
            pltpu.VMEM((nseq, per, 8, half), BF16),
            pltpu.VMEM((nhead, nc, 1, Q), F32),
            dma((3, IN_PIECES)),
            dma((6,)),
            dma((2,)), dma((2,)),
            dma((nseq,)), dma((nseq,)),
            dma((nseq,)), dma((nseq,)),
            dma((nseq,)), dma((nseq,)),
            dma((nhead, groups)), dma((nhead, groups)),
        ],
        compiler_params=pltpu.CompilerParams(
            collective_id=0, has_side_effects=True, vmem_limit_bytes=VMEM_LIMIT
        ),
        name="mamba",
    )(
        *(
            pltpu.with_memory_space_constraint(a, pltpu.HBM)
            for a in (x_in, bc_in, gate_in, log_decay, step_size, conv_x, conv_bc, skip_gain, norm_gain)
        )
    )


def solution(mesh):
    in_specs = (
        P("seq", "head"),
        P("seq", None),
        P("seq", "head"),
        P("head", "seq"),
        P("head", "seq"),
        P(None, "head"),
        P(),
        P("head"),
        P("head"),
    )
    return jax.shard_map(
        functools.partial(per_device, mesh.shape["seq"], mesh.shape["head"]),
        mesh=mesh,
        in_specs=in_specs,
        out_specs=P("seq", "head"),
        check_vma=False,
    )
```
